32 devices in a mesh: batch: 4 (over z), ctx: 2 (over x), tp: 4 (over y, core).
Axes of the slice: x: 2, y: 2, z: 4, core: 2. Of those that a mesh axis runs over, the one named last changes fastest.
Arguments:
- hits: bfloat16 [2048, 1024], P(('batch', 'ctx'), 'tp'), parts along dimension 0, may hold values from -12 to 12
- qkv_weight: bfloat16 [1024, 3, 1024], P(None, None, 'tp'), may hold values from -0.75 to 0.75
- out_weight: bfloat16 [1024, 1024], P('tp'), may hold values from -0.1875 to 0.1875
- energy_order: int32 [2048], P('batch'), parts along dimension 0, may hold values from 0 to 511, as said below
- stripe_owner: int32 [8, 2], P('batch'), parts along dimension 0, may hold values from 0 to 3, as said below
Outputs:
- mixed: bfloat16 [8, 256, 1024], P(('batch', 'ctx'), 'tp'), parts along dimension 0
The draws below stay inside these ranges and needn't reach their ends.
There are 4 independent parts, one for each index of `batch`. The reference program is written for one: setup_inputs(seed, part) draws one part's arguments, and reference() takes and returns one part's arrays. A program takes and returns all parts, laid end to end along the dimension named above; an argument that names none is the same for every part. Nothing has to cross between parts.
Inputs may be any that keep to these rules, and one draw needn't show every extreme that they name: `energy_order`: a permutation of the 512 detector rows; every stripe of 128 consecutive energy positions holds exactly 64 hits of each block of 256 consecutive detector rows. `stripe_owner`: each row holds two stripes a and 3 - a, in either order; every stripe appears exactly once.
All inputs are finite; a program needn't handle non-finite values.
Results may differ from the reference program's by a relative error of at most 0.012.
The reference program's roundings to bfloat16 on the way count: a program that leaves them out, or rounds other values in their place, can miss the bound.
Values may be sent and summed in bfloat16 or wider, within the bound.
A program may use at most 64 MiB of HBM per device.

```python
import math
import jax
import jax.numpy as jnp
from jax import lax

D = 1024
HEADS = 16
HEAD_DIM = 64
TOK_DEV = 256
SEQ = 512
N_CTX = 2


def draw_energy_order(key, part):
    count_ctx = SEQ // TOK_DEV
    stripes = 2 * count_ctx
    per_stripe = TOK_DEV // stripes
    first_key, second_key = jax.random.split(key)
    sources = jnp.repeat(jnp.arange(count_ctx, dtype=jnp.int32), per_stripe)
    stripe_sources = jax.vmap(lambda sub_key: jax.random.permutation(sub_key, sources))(jax.random.split(first_key, stripes))
    onehot = (stripe_sources[:, :, None] == jnp.arange(count_ctx, dtype=jnp.int32)[None, None, :]).astype(jnp.int32)
    ranks = jnp.sum((jnp.cumsum(onehot, axis=1) - 1) * onehot, axis=2)
    local_orders = jax.vmap(lambda sub_key: jax.random.permutation(sub_key, TOK_DEV))(jax.random.split(second_key, count_ctx))
    stripe_ids = jnp.arange(stripes, dtype=jnp.int32)[:, None]
    local_rows = local_orders[stripe_sources, stripe_ids * per_stripe + ranks]
    return (stripe_sources * TOK_DEV + local_rows).reshape(-1).astype(jnp.int32)


def draw_stripe_owner(key, part):
    count_ctx = SEQ // TOK_DEV
    pair_key = jax.random.fold_in(key, 40503)
    flip_key = jax.random.fold_in(key, 91019)
    pairs = jax.random.permutation(pair_key, count_ctx).astype(jnp.int32)
    flips = jax.random.bits(flip_key, (count_ctx,), jnp.uint32) % 2
    first_stripe = jnp.where(flips == 1, 2 * count_ctx - 1 - pairs, pairs)
    second_stripe = 2 * count_ctx - 1 - first_stripe
    return jnp.stack([first_stripe, second_stripe], axis=1).astype(jnp.int32)


def draw_hits(key, part):
    first_key = jax.random.fold_in(key, 0)
    values = jnp.clip(jax.random.normal(first_key, (SEQ, D), jnp.float32), -6.0, 6.0)
    return values.astype(jnp.bfloat16)


def steps_of(own_key, dims, shards, low, largest):
    loudness, own = 1.0, jax.random.fold_in(own_key, 6)
    for position, parts in shards:
        draws = jnp.exp(jax.random.uniform(jax.random.fold_in(own, position), (parts,), jnp.float32, low / len(shards), largest / len(shards)))
        loudness = loudness * jnp.repeat(draws, dims[position] // parts).reshape([-1 if axis == position else 1 for axis in range(len(dims))])
    return loudness


def noise(own_key, shape, spread, limit, cuts=(), kind=jnp.bfloat16):
    factor_of = steps_of(own_key, shape, cuts, -0.22, 0.18) if cuts else 1.0
    values = jax.random.normal(own_key, shape, jnp.float32) * spread * factor_of
    return jnp.minimum(jnp.maximum(values, -limit), limit).astype(kind)


def setup_inputs(seed: int = 0, part: int = 0) -> dict:
    streams_of = jax.random.split(jax.random.key(seed), 6)
    own_keys = jax.random.split(jax.random.fold_in(streams_of[5], part), 6)
    return {
        "hits": draw_hits(jax.random.fold_in(jax.random.fold_in(streams_of[5], part), 71), part),
        "qkv_weight": noise(streams_of[1], (D, 3, D), (1.6 / D ** 0.5), 0.75, ((2, 4),)),
        "out_weight": noise(streams_of[2], (D, D), D ** -0.5, 0.1875, ((0, 4),)),
        "energy_order": draw_energy_order(jax.random.fold_in(jax.random.fold_in(streams_of[5], part), 71), part),
        "stripe_owner": draw_stripe_owner(jax.random.fold_in(jax.random.fold_in(streams_of[5], part), 71), part),
    }


floor_score = -1e+30

def reference(hits, qkv_weight, out_weight, energy_order, stripe_owner):
    seq_len = hits.shape[0]
    rows_dev = seq_len // N_CTX
    ordered = hits[energy_order]
    projected = jnp.dot(ordered, qkv_weight.reshape(D, 3 * D), preferred_element_type=jnp.float32).astype(jnp.bfloat16)
    projected = lax.optimization_barrier(projected).reshape(seq_len, 3, HEADS, HEAD_DIM)
    queries = projected[:, 0]
    key_rows = projected[:, 1].astype(jnp.float32)
    value_rows = projected[:, 2].astype(jnp.float32)
    positions = jnp.arange(seq_len, dtype=jnp.int32)
    block_rows = 256 if seq_len % 256 == 0 else seq_len
    score_scale = 1.0 / math.sqrt(HEAD_DIM)

    def attend_block(offset):
        query_block = lax.dynamic_slice_in_dim(queries, offset, block_rows, 0).astype(jnp.float32)
        scores = jnp.einsum('qhe,khe->hqk', query_block, key_rows) * score_scale
        allowed = positions[None, :] <= (offset + jnp.arange(block_rows, dtype=jnp.int32))[:, None]
        scores = jnp.where(allowed[None], scores, floor_score)
        row_max = lax.optimization_barrier(jnp.max(scores, axis=-1))
        weights = jnp.where(allowed[None], jnp.exp(scores - row_max[:, :, None]), 0.0)
        row_total = lax.optimization_barrier(jnp.sum(weights, axis=-1))
        rounded = lax.optimization_barrier(weights.astype(jnp.bfloat16)).astype(jnp.float32)
        summed = jnp.einsum('hqk,khe->qhe', rounded, value_rows)
        return (summed / jnp.transpose(row_total)[:, :, None]).astype(jnp.bfloat16)
    starts = jnp.arange(seq_len // block_rows, dtype=jnp.int32) * block_rows
    attended = lax.map(attend_block, starts).reshape(seq_len, D)
    layer = jnp.dot(attended, out_weight, preferred_element_type=jnp.float32).astype(jnp.bfloat16)
    stripe_len = rows_dev // 2
    offsets = jnp.arange(stripe_len, dtype=jnp.int32)
    first_rows = stripe_owner[:, 0][:, None] * stripe_len + offsets[None, :]
    second_rows = stripe_owner[:, 1][:, None] * stripe_len + offsets[None, :]
    return layer[jnp.concatenate([first_rows, second_rows], axis=1)]
```

```python
import math

import jax
import jax.numpy as jnp
from jax import lax
from jax.experimental import pallas as pl
from jax.experimental.pallas import tpu as pltpu
from jax.sharding import PartitionSpec as P

HEAD_DIM = 64


floor_score = -1e30


def passed_along(shard, axis, by):
    peers = lax.axis_size(axis)
    return lax.ppermute(shard, axis, [(i, (i + by) % peers) for i in range(peers)])


def stripe_rows(owners, rows_dev, stripes):
    stripe_len = rows_dev // 2
    offsets = jnp.arange(stripe_len, dtype=jnp.int32)
    low_rows = owners[:, None] * stripe_len + offsets[None, :]
    high_rows = (stripes - 1 - owners)[:, None] * stripe_len + offsets[None, :]
    return jnp.concatenate([low_rows, high_rows], axis=1)


def routing(energy_order, pair_owner, my_index, rows_dev, count_ctx):
    every_row = stripe_rows(pair_owner, rows_dev, 2 * count_ctx)
    detector = energy_order[every_row]
    source = detector // rows_dev
    chosen = (source == my_index).astype(jnp.int32)
    ranked = jnp.cumsum(chosen, axis=1) - 1
    per_pair = rows_dev // count_ctx
    slot_ids = jnp.arange(per_pair, dtype=jnp.int32)
    matched = (chosen[:, None, :] == 1) & (ranked[:, None, :] == slot_ids[None, :, None])
    send_rows = jnp.sum(jnp.where(matched, (detector % rows_dev)[:, None, :], 0), axis=-1)
    my_positions = lax.dynamic_index_in_dim(every_row, my_index, 0, keepdims=False)
    mine_source = energy_order[my_positions] // rows_dev
    onehot = (mine_source[:, None] == jnp.arange(count_ctx, dtype=jnp.int32)[None, :]).astype(
        jnp.int32
    )
    mine_rank = jnp.sum((jnp.cumsum(onehot, axis=0) - 1) * onehot, axis=1)
    return (send_rows.reshape(-1), mine_source * per_pair + mine_rank, my_positions)


def empty_state(heads_dev, count_rows):
    return (
        jnp.full((heads_dev, count_rows), floor_score, jnp.float32),
        jnp.zeros((heads_dev, count_rows), jnp.float32),
        jnp.zeros((count_rows, heads_dev, HEAD_DIM), jnp.float32),
    )


def absorb(state_now, queries, key_rows, value_rows, allowed, score_scale):
    running_max, running_sum, running_acc = state_now
    scores = (
        jnp.einsum("qhe,khe->hqk", queries, key_rows, preferred_element_type=jnp.float32)
        * score_scale
    )
    if allowed is not None:
        scores = jnp.where(allowed[None], scores, floor_score)
    new_max = jnp.maximum(running_max, jnp.max(scores, axis=-1))
    weights = jnp.exp(scores - new_max[:, :, None])
    if allowed is not None:
        weights = jnp.where(allowed[None], weights, 0.0)
    shrink = jnp.exp(running_max - new_max)
    new_sum = running_sum * shrink + jnp.sum(weights, axis=-1)
    added = jnp.einsum(
        "hqk,khe->qhe", weights.astype(jnp.bfloat16), value_rows, preferred_element_type=jnp.float32
    )
    new_acc = running_acc * jnp.transpose(shrink)[:, :, None] + added
    return (new_max, new_sum, new_acc)


def finish(state_now):
    return state_now[2] / jnp.transpose(state_now[1])[:, :, None]


def shards(hits, qkv_weight, out_weight, energy_order, stripe_owner):
    rows_dev, width_dev = hits.shape
    model_width = qkv_weight.shape[0]
    count_ctx = lax.axis_size("ctx")
    my_index = lax.axis_index("ctx")
    heads_dev = width_dev // HEAD_DIM
    score_scale = 1.0 / math.sqrt(HEAD_DIM)
    stripe_len = rows_dev // 2
    per_pair = rows_dev // count_ctx
    pair_owner = jnp.minimum(stripe_owner[:, 0], stripe_owner[:, 1])
    send_rows, take_rows, my_positions = routing(
        energy_order, pair_owner, my_index, rows_dev, count_ctx
    )
    flat_weight = qkv_weight.reshape(model_width, 3 * width_dev)
    outgoing = hits[send_rows].reshape(count_ctx, per_pair, width_dev)
    incoming = lax.all_to_all(outgoing, "ctx", split_axis=0, concat_axis=0, tiled=True)
    arranged = incoming.reshape(count_ctx * per_pair, width_dev)[take_rows]
    projected = jnp.dot(
        lax.all_gather(arranged, "tp", axis=1, tiled=True),
        flat_weight,
        preferred_element_type=jnp.float32,
    ).astype(jnp.bfloat16)
    queries = projected[:, :width_dev].reshape(rows_dev, heads_dev, HEAD_DIM)
    key_value = projected[:, width_dev:]
    low_queries = queries[:stripe_len]
    high_queries = queries[stripe_len:]

    def split_pair(pair_block):
        count_rows = pair_block.shape[0]
        return (
            pair_block[:, :width_dev].reshape(count_rows, heads_dev, HEAD_DIM),
            pair_block[:, width_dev:].reshape(count_rows, heads_dev, HEAD_DIM),
        )

    my_stripe = pair_owner[my_index]
    own_keys, own_values = split_pair(key_value)
    low_allowed = my_positions[None, :stripe_len] <= my_positions[:stripe_len, None]
    high_allowed = my_positions[None, :] <= my_positions[stripe_len:, None]
    low_state = absorb(
        empty_state(heads_dev, stripe_len),
        low_queries,
        own_keys[:stripe_len],
        own_values[:stripe_len],
        low_allowed,
        score_scale,
    )
    high_state = absorb(
        empty_state(heads_dev, stripe_len),
        high_queries,
        own_keys,
        own_values,
        high_allowed,
        score_scale,
    )

    def advance(turn_index, state_now):
        pair_block, low_now, high_now = state_now
        pair_block = passed_along(pair_block, "ctx", 1)
        sender = (my_index - turn_index) % count_ctx
        their_stripe = pair_owner[sender]
        key_rows, value_rows = split_pair(pair_block)
        high_now = absorb(
            high_now,
            high_queries,
            key_rows[:stripe_len],
            value_rows[:stripe_len],
            None,
            score_scale,
        )

        def lower_first():
            return (
                absorb(
                    low_now,
                    low_queries,
                    key_rows[:stripe_len],
                    value_rows[:stripe_len],
                    None,
                    score_scale,
                ),
                high_now,
            )

        def upper_first():
            return (
                low_now,
                absorb(
                    high_now,
                    high_queries,
                    key_rows[stripe_len:],
                    value_rows[stripe_len:],
                    None,
                    score_scale,
                ),
            )

        low_now, high_now = lax.cond(their_stripe < my_stripe, lower_first, upper_first)
        return (pair_block, low_now, high_now)

    moved_block, low_state, high_state = lax.fori_loop(
        1, count_ctx, advance, (key_value, low_state, high_state)
    )
    attended = jnp.concatenate([finish(low_state), finish(high_state)], axis=0)
    merged = attended.astype(jnp.bfloat16).reshape(rows_dev, width_dev)
    my_pair = stripe_owner[my_index]
    swapped = my_pair[0] > my_pair[1]
    merged = jnp.where(swapped, jnp.roll(merged, stripe_len, axis=0), merged)
    mixed = lax.psum_scatter(
        jnp.dot(merged, out_weight, preferred_element_type=jnp.float32).astype(jnp.bfloat16),
        "tp",
        scatter_dimension=0,
        tiled=True,
    )
    return mixed[None]


def layer_kernel(
    hits_ref,
    qkv_ref,
    wout_ref,
    order_ref,
    owner_ref,
    out_ref,
    gath,
    wq,
    wmine,
    wtheirs,
    acc,
    proj,
    pick,
    bias,
    qrows,
    att_send,
    att_recv,
    far_send,
    far_recv,
    near,
    local_sem,
    send_sem,
    gath_sem,
    wout_sem,
    att_sem,
    far_sem,
):
    i = lax.axis_index("ctx")
    t = lax.axis_index("tp")
    y = t // 2
    c = t % 2
    oi, oy = 1 - i, 1 - y
    rows, width = hits_ref.shape
    seq = 2 * rows
    half = rows // 2
    quarter = rows // 4
    heads = width // HEAD_DIM
    score_scale = 1.0 / math.sqrt(HEAD_DIM)
    partner = {"ctx": i, "tp": 2 * y + 1 - c}
    x_peer = {"ctx": oi, "tp": t}
    y_peer = {"ctx": i, "tp": 2 * oy + c}
    t_partner = 2 * y + 1 - c
    t_y = 2 * oy + c
    t_diag_partner = 2 * oy + 1 - c

    local = []

    def local_copy(src, dst):
        copy = pltpu.make_async_copy(src, dst, local_sem.at[len(local)])
        copy.start()
        local.append(copy)
        return copy

    hits_in = local_copy(hits_ref, gath.at[i, t])
    weight_in = [
        [
            local_copy(
                qkv_ref.at[j, pl.ds(part * 2 * width, 2 * width)],
                wq.at[j, pl.ds(part * 2 * width, 2 * width)],
            )
            for j in range(3)
        ]
        for part in (y, oy)
    ]
    wout_in = local_copy(wout_ref, wmine)

    barrier = pltpu.get_barrier_semaphore()
    for peer in (partner, x_peer, y_peer):
        pl.semaphore_signal(
            barrier, inc=1, device_id=peer, device_id_type=pl.DeviceIdType.MESH
        )
    pl.semaphore_wait(barrier, 3)

    sent = []

    def remote(src, dst, recv, peer):
        copy = pltpu.make_async_remote_copy(
            src_ref=src,
            dst_ref=dst,
            send_sem=send_sem.at[len(sent)],
            recv_sem=recv,
            device_id=peer,
            device_id_type=pl.DeviceIdType.MESH,
        )
        copy.start()
        sent.append(copy)

    def arrived(dst, recv):
        pltpu.make_async_remote_copy(
            src_ref=dst,
            dst_ref=dst,
            send_sem=send_sem.at[0],
            recv_sem=recv,
            device_id=partner,
            device_id_type=pl.DeviceIdType.MESH,
        ).wait_recv()

    def slot(ci, ti, h):
        return gath.at[ci, ti, pl.ds(h * half, half)]

    def own_to(h, peer):
        remote(hits_ref.at[pl.ds(h * half, half)], slot(i, t, h), gath_sem.at[i, t, h], peer)

    def forward(ci, ti, h, peer):
        remote(slot(ci, ti, h), slot(ci, ti, h), gath_sem.at[ci, ti, h], peer)

    def got(ci, ti, h):
        arrived(slot(ci, ti, h), gath_sem.at[ci, ti, h])

    own_to(0, x_peer)
    own_to(1, y_peer)
    own_to(0, partner)
    own_to(1, partner)
    own_to(1, x_peer)
    own_to(0, y_peer)
    remote(wout_ref, wtheirs, wout_sem.at[0], partner)

    order = order_ref[...].astype(jnp.float32)
    order_rows = jnp.transpose(jnp.broadcast_to(order, (128, seq)))
    entry = lax.broadcasted_iota(jnp.int32, (seq, 128), 0).astype(jnp.float32)
    lane = lax.broadcasted_iota(jnp.int32, (seq, 128), 1)
    row = lax.broadcasted_iota(jnp.int32, (rows, 128), 0)
    first, second = owner_ref[i, 0], owner_ref[i, 1]
    mine_pos = jnp.where(row < half, first * half + row, second * half + row - half).astype(
        jnp.float32
    )
    for block in range(seq // 128):
        cols = pl.ds(block * 128, 128)
        detector = (lane + block * 128).astype(jnp.float32)
        pos = jnp.sum(jnp.where(order_rows == detector, entry, 0.0), axis=0, keepdims=True)
        bias[:, cols] = jnp.where(pos <= mine_pos, 0.0, floor_score)
        pick[:, cols] = jnp.where(pos == mine_pos, score_scale, 0.0).astype(jnp.bfloat16)

    def partial(ci, part, j):
        left = jnp.concatenate([gath[ci, 2 * part], gath[ci, 2 * part + 1]], axis=1)
        right = wq[j, pl.ds(pl.multiple_of(part * 2 * width, 2 * width), 2 * width), :]
        return jnp.dot(left, right, preferred_element_type=jnp.float32)

    def open_rows(ci, which):
        for j in range(3):
            acc[which, j] = partial(ci, y, j)

    def close_rows(ci, which):
        for j in range(3):
            proj[j, pl.ds(pl.multiple_of(ci * rows, rows), rows), :] = (
                acc[which, j] + partial(ci, oy, j)
            ).astype(jnp.bfloat16)

    hits_in.wait()
    for copy in weight_in[0]:
        copy.wait()
    got(i, t_partner, 0)
    got(i, t_partner, 1)
    open_rows(i, 0)

    got(oi, t, 0)
    forward(oi, t, 0, y_peer)
    forward(oi, t, 0, partner)
    got(i, t_y, 1)
    forward(i, t_y, 1, x_peer)
    forward(i, t_y, 1, partner)
    got(oi, t, 1)
    forward(oi, t, 1, partner)
    got(i, t_y, 0)
    forward(i, t_y, 0, partner)

    got(oi, t_partner, 0)
    got(oi, t_partner, 1)
    open_rows(oi, 1)

    got(oi, t_y, 0)
    forward(oi, t_y, 0, partner)
    got(oi, t_y, 1)
    forward(oi, t_y, 1, partner)

    for copy in weight_in[1]:
        copy.wait()
    got(i, t_diag_partner, 0)
    got(i, t_diag_partner, 1)
    close_rows(i, 0)
    got(oi, t_diag_partner, 0)
    got(oi, t_diag_partner, 1)
    close_rows(oi, 1)

    qrows[...] = jnp.dot(pick[...], proj[0], preferred_element_type=jnp.float32)
    head_of = lax.broadcasted_iota(jnp.int32, (quarter, width), 1) // HEAD_DIM

    def attend(owner):
        start = pl.multiple_of(owner * quarter, quarter)
        queries = qrows[pl.ds(start, quarter), :]
        spread = jnp.concatenate(
            [jnp.where(head_of == h, queries, 0.0) for h in range(heads)], axis=0
        ).astype(jnp.bfloat16)
        scores = lax.dot_general(
            spread, proj[1], (((1,), (1,)), ((), ())), preferred_element_type=jnp.float32
        )
        allowed = bias[pl.ds(start, quarter), :]
        scores = scores + jnp.concatenate([allowed] * heads, axis=0)
        weights = jnp.exp(scores - jnp.max(scores, axis=1, keepdims=True))
        total = jnp.sum(weights, axis=1, keepdims=True)
        summed = jnp.dot(
            weights.astype(jnp.bfloat16), proj[2], preferred_element_type=jnp.float32
        ) / total
        merged = jnp.zeros((quarter, width), jnp.float32)
        for h in range(heads):
            merged = jnp.where(head_of == h, summed[h * quarter : (h + 1) * quarter], merged)
        return merged.astype(jnp.bfloat16)

    att_send[0] = attend(t_diag_partner)
    remote(att_send.at[0], att_recv.at[0], att_sem.at[0], partner)
    far_mine = attend(t_y)
    wout_in.wait()
    far_part = jnp.dot(far_mine, wmine[...], preferred_element_type=jnp.float32)
    arrived(wtheirs, wout_sem.at[0])
    arrived(att_recv.at[0], att_sem.at[0])
    far_send[...] = (
        far_part + jnp.dot(att_recv[0], wtheirs[...], preferred_element_type=jnp.float32)
    ).astype(jnp.bfloat16)
    remote(far_send, far_recv, far_sem.at[0], y_peer)

    att_send[1] = attend(t_partner)
    remote(att_send.at[1], att_recv.at[1], att_sem.at[1], partner)
    near[...] = jnp.dot(attend(t), wmine[...], preferred_element_type=jnp.float32)
    arrived(att_recv.at[1], att_sem.at[1])
    near[...] += jnp.dot(att_recv[1], wtheirs[...], preferred_element_type=jnp.float32)
    arrived(far_recv, far_sem.at[0])
    out_ref[...] = (near[...] + far_recv[...].astype(jnp.float32)).astype(jnp.bfloat16)
    for copy in sent:
        copy.wait_send()


def small_slice(hits, qkv_weight, out_weight, energy_order, stripe_owner):
    rows, width = hits.shape
    model_width = qkv_weight.shape[0]
    bf16, f32 = jnp.bfloat16, jnp.float32
    dma = pltpu.SemaphoreType.DMA
    anywhere = pl.BlockSpec(memory_space=pl.ANY)
    mixed = pl.pallas_call(
        layer_kernel,
        out_shape=jax.ShapeDtypeStruct((rows // 4, model_width), bf16),
        in_specs=[
            anywhere,
            anywhere,
            anywhere,
            pl.BlockSpec(memory_space=pltpu.VMEM),
            pl.BlockSpec(memory_space=pltpu.SMEM),
        ],
        out_specs=pl.BlockSpec(memory_space=pltpu.VMEM),
        scratch_shapes=[
            pltpu.VMEM((2, 4, rows, width), bf16),
            pltpu.VMEM((3, model_width, width), bf16),
            pltpu.VMEM((width, model_width), bf16),
            pltpu.VMEM((width, model_width), bf16),
            pltpu.VMEM((2, 3, rows, width), f32),
            pltpu.VMEM((3, 2 * rows, width), bf16),
            pltpu.VMEM((rows, 2 * rows), bf16),
            pltpu.VMEM((rows, 2 * rows), f32),
            pltpu.VMEM((rows, width), f32),
            pltpu.VMEM((2, rows // 4, width), bf16),
            pltpu.VMEM((2, rows // 4, width), bf16),
            pltpu.VMEM((rows // 4, model_width), bf16),
            pltpu.VMEM((rows // 4, model_width), bf16),
            pltpu.VMEM((rows // 4, model_width), f32),
            dma((8,)),
            dma((18,)),
            dma((2, 4, 2)),
            dma((1,)),
            dma((2,)),
            dma((1,)),
        ],
        compiler_params=pltpu.CompilerParams(
            collective_id=0, has_side_effects=True, vmem_limit_bytes=40 * 1024 * 1024
        ),
    )(
        hits,
        jnp.transpose(qkv_weight, (1, 0, 2)),
        out_weight,
        energy_order.reshape(1, -1),
        stripe_owner,
    )
    return mixed[None]


def solution(mesh):
    small = mesh.shape["ctx"] == 2 and mesh.shape["tp"] == 4
    placed = (
        P(("batch", "ctx"), "tp"),
        P(None, None, "tp"),
        P("tp", None),
        P("batch"),
        P("batch", None),
    )
    return jax.shard_map(
        small_slice if small else shards,
        mesh=mesh,
        in_specs=placed,
        out_specs=P(("batch", "ctx"), "tp", None),
        check_vma=False,
    )
```

```python
import math

import jax
import jax.numpy as jnp
from jax import lax
from jax.experimental import pallas as pl
from jax.experimental.pallas import tpu as pltpu
from jax.sharding import PartitionSpec as P

HEAD_DIM = 64


floor_score = -1e30


def passed_along(shard, axis, by):
    peers = lax.axis_size(axis)
    return lax.ppermute(shard, axis, [(i, (i + by) % peers) for i in range(peers)])


def stripe_rows(owners, rows_dev, stripes):
    stripe_len = rows_dev // 2
    offsets = jnp.arange(stripe_len, dtype=jnp.int32)
    low_rows = owners[:, None] * stripe_len + offsets[None, :]
    high_rows = (stripes - 1 - owners)[:, None] * stripe_len + offsets[None, :]
    return jnp.concatenate([low_rows, high_rows], axis=1)


def routing(energy_order, pair_owner, my_index, rows_dev, count_ctx):
    every_row = stripe_rows(pair_owner, rows_dev, 2 * count_ctx)
    detector = energy_order[every_row]
    source = detector // rows_dev
    chosen = (source == my_index).astype(jnp.int32)
    ranked = jnp.cumsum(chosen, axis=1) - 1
    per_pair = rows_dev // count_ctx
    slot_ids = jnp.arange(per_pair, dtype=jnp.int32)
    matched = (chosen[:, None, :] == 1) & (ranked[:, None, :] == slot_ids[None, :, None])
    send_rows = jnp.sum(jnp.where(matched, (detector % rows_dev)[:, None, :], 0), axis=-1)
    my_positions = lax.dynamic_index_in_dim(every_row, my_index, 0, keepdims=False)
    mine_source = energy_order[my_positions] // rows_dev
    onehot = (mine_source[:, None] == jnp.arange(count_ctx, dtype=jnp.int32)[None, :]).astype(
        jnp.int32
    )
    mine_rank = jnp.sum((jnp.cumsum(onehot, axis=0) - 1) * onehot, axis=1)
    return (send_rows.reshape(-1), mine_source * per_pair + mine_rank, my_positions)


def empty_state(heads_dev, count_rows):
    return (
        jnp.full((heads_dev, count_rows), floor_score, jnp.float32),
        jnp.zeros((heads_dev, count_rows), jnp.float32),
        jnp.zeros((count_rows, heads_dev, HEAD_DIM), jnp.float32),
    )


def absorb(state_now, queries, key_rows, value_rows, allowed, score_scale):
    running_max, running_sum, running_acc = state_now
    scores = (
        jnp.einsum("qhe,khe->hqk", queries, key_rows, preferred_element_type=jnp.float32)
        * score_scale
    )
    if allowed is not None:
        scores = jnp.where(allowed[None], scores, floor_score)
    new_max = jnp.maximum(running_max, jnp.max(scores, axis=-1))
    weights = jnp.exp(scores - new_max[:, :, None])
    if allowed is not None:
        weights = jnp.where(allowed[None], weights, 0.0)
    shrink = jnp.exp(running_max - new_max)
    new_sum = running_sum * shrink + jnp.sum(weights, axis=-1)
    added = jnp.einsum(
        "hqk,khe->qhe", weights.astype(jnp.bfloat16), value_rows, preferred_element_type=jnp.float32
    )
    new_acc = running_acc * jnp.transpose(shrink)[:, :, None] + added
    return (new_max, new_sum, new_acc)


def finish(state_now):
    return state_now[2] / jnp.transpose(state_now[1])[:, :, None]


def shards(hits, qkv_weight, out_weight, energy_order, stripe_owner):
    rows_dev, width_dev = hits.shape
    model_width = qkv_weight.shape[0]
    count_ctx = lax.axis_size("ctx")
    my_index = lax.axis_index("ctx")
    heads_dev = width_dev // HEAD_DIM
    score_scale = 1.0 / math.sqrt(HEAD_DIM)
    stripe_len = rows_dev // 2
    per_pair = rows_dev // count_ctx
    pair_owner = jnp.minimum(stripe_owner[:, 0], stripe_owner[:, 1])
    send_rows, take_rows, my_positions = routing(
        energy_order, pair_owner, my_index, rows_dev, count_ctx
    )
    flat_weight = qkv_weight.reshape(model_width, 3 * width_dev)
    outgoing = hits[send_rows].reshape(count_ctx, per_pair, width_dev)
    incoming = lax.all_to_all(outgoing, "ctx", split_axis=0, concat_axis=0, tiled=True)
    arranged = incoming.reshape(count_ctx * per_pair, width_dev)[take_rows]
    projected = jnp.dot(
        lax.all_gather(arranged, "tp", axis=1, tiled=True),
        flat_weight,
        preferred_element_type=jnp.float32,
    ).astype(jnp.bfloat16)
    queries = projected[:, :width_dev].reshape(rows_dev, heads_dev, HEAD_DIM)
    key_value = projected[:, width_dev:]
    low_queries = queries[:stripe_len]
    high_queries = queries[stripe_len:]

    def split_pair(pair_block):
        count_rows = pair_block.shape[0]
        return (
            pair_block[:, :width_dev].reshape(count_rows, heads_dev, HEAD_DIM),
            pair_block[:, width_dev:].reshape(count_rows, heads_dev, HEAD_DIM),
        )

    my_stripe = pair_owner[my_index]
    own_keys, own_values = split_pair(key_value)
    low_allowed = my_positions[None, :stripe_len] <= my_positions[:stripe_len, None]
    high_allowed = my_positions[None, :] <= my_positions[stripe_len:, None]
    low_state = absorb(
        empty_state(heads_dev, stripe_len),
        low_queries,
        own_keys[:stripe_len],
        own_values[:stripe_len],
        low_allowed,
        score_scale,
    )
    high_state = absorb(
        empty_state(heads_dev, stripe_len),
        high_queries,
        own_keys,
        own_values,
        high_allowed,
        score_scale,
    )

    def advance(turn_index, state_now):
        pair_block, low_now, high_now = state_now
        pair_block = passed_along(pair_block, "ctx", 1)
        sender = (my_index - turn_index) % count_ctx
        their_stripe = pair_owner[sender]
        key_rows, value_rows = split_pair(pair_block)
        high_now = absorb(
            high_now,
            high_queries,
            key_rows[:stripe_len],
            value_rows[:stripe_len],
            None,
            score_scale,
        )

        def lower_first():
            return (
                absorb(
                    low_now,
                    low_queries,
                    key_rows[:stripe_len],
                    value_rows[:stripe_len],
                    None,
                    score_scale,
                ),
                high_now,
            )

        def upper_first():
            return (
                low_now,
                absorb(
                    high_now,
                    high_queries,
                    key_rows[stripe_len:],
                    value_rows[stripe_len:],
                    None,
                    score_scale,
                ),
            )

        low_now, high_now = lax.cond(their_stripe < my_stripe, lower_first, upper_first)
        return (pair_block, low_now, high_now)

    moved_block, low_state, high_state = lax.fori_loop(
        1, count_ctx, advance, (key_value, low_state, high_state)
    )
    attended = jnp.concatenate([finish(low_state), finish(high_state)], axis=0)
    merged = attended.astype(jnp.bfloat16).reshape(rows_dev, width_dev)
    my_pair = stripe_owner[my_index]
    swapped = my_pair[0] > my_pair[1]
    merged = jnp.where(swapped, jnp.roll(merged, stripe_len, axis=0), merged)
    mixed = lax.psum_scatter(
        jnp.dot(merged, out_weight, preferred_element_type=jnp.float32).astype(jnp.bfloat16),
        "tp",
        scatter_dimension=0,
        tiled=True,
    )
    return mixed[None]


def layer_kernel(
    hits_ref,
    qkv_ref,
    wout_ref,
    order_hbm,
    owner_hbm,
    out_ref,
    order_ref,
    owner_ref,
    gath,
    wq,
    wmine,
    wtheirs,
    acc,
    proj,
    pick,
    bias,
    qrows,
    att_send,
    att_recv,
    far_send,
    far_recv,
    near,
    local_sem,
    send_sem,
    gath_sem,
    wout_sem,
    att_sem,
    far_sem,
):
    i = lax.axis_index("ctx")
    t = lax.axis_index("tp")
    y = t // 2
    c = t % 2
    oi, oy = 1 - i, 1 - y
    rows, width = hits_ref.shape
    seq = 2 * rows
    half = rows // 2
    quarter = rows // 4
    heads = width // HEAD_DIM
    score_scale = 1.0 / math.sqrt(HEAD_DIM)
    partner = {"ctx": i, "tp": 2 * y + 1 - c}
    x_peer = {"ctx": oi, "tp": t}
    y_peer = {"ctx": i, "tp": 2 * oy + c}
    t_partner = 2 * y + 1 - c
    t_y = 2 * oy + c
    t_diag_partner = 2 * oy + 1 - c

    local = []

    def local_copy(src, dst):
        copy = pltpu.make_async_copy(src, dst, local_sem.at[len(local)])
        copy.start()
        local.append(copy)
        return copy

    hits_in = local_copy(hits_ref, gath.at[i, t])
    order_in = local_copy(order_hbm, order_ref)
    owner_in = local_copy(owner_hbm, owner_ref)
    weight_in = [
        [
            local_copy(
                qkv_ref.at[j, pl.ds(part * 2 * width, 2 * width)],
                wq.at[j, pl.ds(part * 2 * width, 2 * width)],
            )
            for j in range(3)
        ]
        for part in (y, oy)
    ]
    wout_in = local_copy(wout_ref, wmine)

    barrier = pltpu.get_barrier_semaphore()
    for peer in (partner, x_peer, y_peer):
        pl.semaphore_signal(
            barrier, inc=1, device_id=peer, device_id_type=pl.DeviceIdType.MESH
        )
    pl.semaphore_wait(barrier, 3)

    sent = []

    def remote(src, dst, recv, peer):
        copy = pltpu.make_async_remote_copy(
            src_ref=src,
            dst_ref=dst,
            send_sem=send_sem.at[len(sent)],
            recv_sem=recv,
            device_id=peer,
            device_id_type=pl.DeviceIdType.MESH,
        )
        copy.start()
        sent.append(copy)

    def arrived(dst, recv):
        pltpu.make_async_remote_copy(
            src_ref=dst,
            dst_ref=dst,
            send_sem=send_sem.at[0],
            recv_sem=recv,
            device_id=partner,
            device_id_type=pl.DeviceIdType.MESH,
        ).wait_recv()

    def slot(ci, ti, h):
        return gath.at[ci, ti, pl.ds(h * half, half)]

    def own_to(h, peer):
        remote(hits_ref.at[pl.ds(h * half, half)], slot(i, t, h), gath_sem.at[i, t, h], peer)

    def forward(ci, ti, h, peer):
        remote(slot(ci, ti, h), slot(ci, ti, h), gath_sem.at[ci, ti, h], peer)

    def got(ci, ti, h):
        arrived(slot(ci, ti, h), gath_sem.at[ci, ti, h])

    own_to(0, x_peer)
    own_to(1, y_peer)
    own_to(0, partner)
    own_to(1, partner)
    own_to(1, x_peer)
    own_to(0, y_peer)
    remote(wout_ref, wtheirs, wout_sem.at[0], partner)

    order_in.wait()
    owner_in.wait()
    order = order_ref[...].astype(jnp.float32)
    order_rows = jnp.transpose(jnp.broadcast_to(order, (128, seq)))
    entry = lax.broadcasted_iota(jnp.int32, (seq, 128), 0).astype(jnp.float32)
    lane = lax.broadcasted_iota(jnp.int32, (seq, 128), 1)
    row = lax.broadcasted_iota(jnp.int32, (rows, 128), 0)
    first, second = owner_ref[i, 0], owner_ref[i, 1]
    mine_pos = jnp.where(row < half, first * half + row, second * half + row - half).astype(
        jnp.float32
    )
    for block in range(seq // 128):
        cols = pl.ds(block * 128, 128)
        detector = (lane + block * 128).astype(jnp.float32)
        pos = jnp.sum(jnp.where(order_rows == detector, entry, 0.0), axis=0, keepdims=True)
        bias[:, cols] = jnp.where(pos <= mine_pos, 0.0, floor_score)
        pick[:, cols] = jnp.where(pos == mine_pos, score_scale, 0.0).astype(jnp.bfloat16)

    def partial(ci, part, j):
        left = jnp.concatenate([gath[ci, 2 * part], gath[ci, 2 * part + 1]], axis=1)
        right = wq[j, pl.ds(pl.multiple_of(part * 2 * width, 2 * width), 2 * width), :]
        return jnp.dot(left, right, preferred_element_type=jnp.float32)

    def open_rows(ci, which):
        for j in range(3):
            acc[which, j] = partial(ci, y, j)

    def close_rows(ci, which):
        for j in range(3):
            proj[j, pl.ds(pl.multiple_of(ci * rows, rows), rows), :] = (
                acc[which, j] + partial(ci, oy, j)
            ).astype(jnp.bfloat16)

    hits_in.wait()
    for copy in weight_in[0]:
        copy.wait()
    got(i, t_partner, 0)
    got(i, t_partner, 1)
    open_rows(i, 0)

    got(oi, t, 0)
    forward(oi, t, 0, y_peer)
    forward(oi, t, 0, partner)
    got(i, t_y, 1)
    forward(i, t_y, 1, x_peer)
    forward(i, t_y, 1, partner)
    got(oi, t, 1)
    forward(oi, t, 1, partner)
    got(i, t_y, 0)
    forward(i, t_y, 0, partner)

    got(oi, t_partner, 0)
    got(oi, t_partner, 1)
    open_rows(oi, 1)

    got(oi, t_y, 0)
    forward(oi, t_y, 0, partner)
    got(oi, t_y, 1)
    forward(oi, t_y, 1, partner)

    for copy in weight_in[1]:
        copy.wait()
    got(i, t_diag_partner, 0)
    got(i, t_diag_partner, 1)
    close_rows(i, 0)
    got(oi, t_diag_partner, 0)
    got(oi, t_diag_partner, 1)
    close_rows(oi, 1)

    qrows[...] = jnp.dot(pick[...], proj[0], preferred_element_type=jnp.float32)
    head_of = lax.broadcasted_iota(jnp.int32, (quarter, width), 1) // HEAD_DIM

    def attend(owner):
        start = pl.multiple_of(owner * quarter, quarter)
        queries = qrows[pl.ds(start, quarter), :]
        spread = jnp.concatenate(
            [jnp.where(head_of == h, queries, 0.0) for h in range(heads)], axis=0
        ).astype(jnp.bfloat16)
        scores = lax.dot_general(
            spread, proj[1], (((1,), (1,)), ((), ())), preferred_element_type=jnp.float32
        )
        allowed = bias[pl.ds(start, quarter), :]
        scores = scores + jnp.concatenate([allowed] * heads, axis=0)
        weights = jnp.exp(scores - jnp.max(scores, axis=1, keepdims=True))
        total = jnp.sum(weights, axis=1, keepdims=True)
        summed = jnp.dot(
            weights.astype(jnp.bfloat16), proj[2], preferred_element_type=jnp.float32
        ) / total
        merged = jnp.zeros((quarter, width), jnp.float32)
        for h in range(heads):
            merged = jnp.where(head_of == h, summed[h * quarter : (h + 1) * quarter], merged)
        return merged.astype(jnp.bfloat16)

    att_send[0] = attend(t_diag_partner)
    remote(att_send.at[0], att_recv.at[0], att_sem.at[0], partner)
    far_mine = attend(t_y)
    wout_in.wait()
    far_part = jnp.dot(far_mine, wmine[...], preferred_element_type=jnp.float32)
    arrived(wtheirs, wout_sem.at[0])
    arrived(att_recv.at[0], att_sem.at[0])
    far_send[...] = (
        far_part + jnp.dot(att_recv[0], wtheirs[...], preferred_element_type=jnp.float32)
    ).astype(jnp.bfloat16)
    remote(far_send, far_recv, far_sem.at[0], y_peer)

    att_send[1] = attend(t_partner)
    remote(att_send.at[1], att_recv.at[1], att_sem.at[1], partner)
    near[...] = jnp.dot(attend(t), wmine[...], preferred_element_type=jnp.float32)
    arrived(att_recv.at[1], att_sem.at[1])
    near[...] += jnp.dot(att_recv[1], wtheirs[...], preferred_element_type=jnp.float32)
    arrived(far_recv, far_sem.at[0])
    out_ref[...] = (near[...] + far_recv[...].astype(jnp.float32)).astype(jnp.bfloat16)
    for copy in sent:
        copy.wait_send()


def small_slice(hits, qkv_weight, out_weight, energy_order, stripe_owner):
    rows, width = hits.shape
    model_width = qkv_weight.shape[0]
    bf16, f32 = jnp.bfloat16, jnp.float32
    dma = pltpu.SemaphoreType.DMA
    in_hbm = pl.BlockSpec(memory_space=pl.ANY)
    mixed = pl.pallas_call(
        layer_kernel,
        out_shape=jax.ShapeDtypeStruct((rows // 4, model_width), bf16),
        in_specs=[
            in_hbm,
            in_hbm,
            in_hbm,
            in_hbm,
            in_hbm,
        ],
        out_specs=pl.BlockSpec(memory_space=pltpu.VMEM),
        scratch_shapes=[
            pltpu.VMEM((1, 2 * rows), jnp.int32),
            pltpu.SMEM((2, 2), jnp.int32),
            pltpu.VMEM((2, 4, rows, width), bf16),
            pltpu.VMEM((3, model_width, width), bf16),
            pltpu.VMEM((width, model_width), bf16),
            pltpu.VMEM((width, model_width), bf16),
            pltpu.VMEM((2, 3, rows, width), f32),
            pltpu.VMEM((3, 2 * rows, width), bf16),
            pltpu.VMEM((rows, 2 * rows), bf16),
            pltpu.VMEM((rows, 2 * rows), f32),
            pltpu.VMEM((rows, width), f32),
            pltpu.VMEM((2, rows // 4, width), bf16),
            pltpu.VMEM((2, rows // 4, width), bf16),
            pltpu.VMEM((rows // 4, model_width), bf16),
            pltpu.VMEM((rows // 4, model_width), bf16),
            pltpu.VMEM((rows // 4, model_width), f32),
            dma((10,)),
            dma((18,)),
            dma((2, 4, 2)),
            dma((1,)),
            dma((2,)),
            dma((1,)),
        ],
        compiler_params=pltpu.CompilerParams(
            collective_id=0, has_side_effects=True, vmem_limit_bytes=67043328
        ),
    )(
        hits,
        jnp.transpose(qkv_weight, (1, 0, 2)),
        out_weight,
        energy_order.reshape(1, -1),
        stripe_owner,
    )
    return mixed[None]


def solution(mesh):
    small = mesh.shape["ctx"] == 2 and mesh.shape["tp"] == 4
    placed = (
        P(("batch", "ctx"), "tp"),
        P(None, None, "tp"),
        P("tp", None),
        P("batch"),
        P("batch", None),
    )
    return jax.shard_map(
        small_slice if small else shards,
        mesh=mesh,
        in_specs=placed,
        out_specs=P(("batch", "ctx"), "tp", None),
        check_vma=False,
    )
```

```python
import math

import jax
import jax.numpy as jnp
from jax import lax
from jax.experimental import pallas as pl
from jax.experimental.pallas import tpu as pltpu
from jax.sharding import PartitionSpec as P

HEAD_DIM = 64


floor_score = -1e30


def passed_along(shard, axis, by):
    peers = lax.axis_size(axis)
    return lax.ppermute(shard, axis, [(i, (i + by) % peers) for i in range(peers)])


def stripe_rows(owners, rows_dev, stripes):
    stripe_len = rows_dev // 2
    offsets = jnp.arange(stripe_len, dtype=jnp.int32)
    low_rows = owners[:, None] * stripe_len + offsets[None, :]
    high_rows = (stripes - 1 - owners)[:, None] * stripe_len + offsets[None, :]
    return jnp.concatenate([low_rows, high_rows], axis=1)


def routing(energy_order, pair_owner, my_index, rows_dev, count_ctx):
    every_row = stripe_rows(pair_owner, rows_dev, 2 * count_ctx)
    detector = energy_order[every_row]
    source = detector // rows_dev
    chosen = (source == my_index).astype(jnp.int32)
    ranked = jnp.cumsum(chosen, axis=1) - 1
    per_pair = rows_dev // count_ctx
    slot_ids = jnp.arange(per_pair, dtype=jnp.int32)
    matched = (chosen[:, None, :] == 1) & (ranked[:, None, :] == slot_ids[None, :, None])
    send_rows = jnp.sum(jnp.where(matched, (detector % rows_dev)[:, None, :], 0), axis=-1)
    my_positions = lax.dynamic_index_in_dim(every_row, my_index, 0, keepdims=False)
    mine_source = energy_order[my_positions] // rows_dev
    onehot = (mine_source[:, None] == jnp.arange(count_ctx, dtype=jnp.int32)[None, :]).astype(
        jnp.int32
    )
    mine_rank = jnp.sum((jnp.cumsum(onehot, axis=0) - 1) * onehot, axis=1)
    return (send_rows.reshape(-1), mine_source * per_pair + mine_rank, my_positions)


def empty_state(heads_dev, count_rows):
    return (
        jnp.full((heads_dev, count_rows), floor_score, jnp.float32),
        jnp.zeros((heads_dev, count_rows), jnp.float32),
        jnp.zeros((count_rows, heads_dev, HEAD_DIM), jnp.float32),
    )


def absorb(state_now, queries, key_rows, value_rows, allowed, score_scale):
    running_max, running_sum, running_acc = state_now
    scores = (
        jnp.einsum("qhe,khe->hqk", queries, key_rows, preferred_element_type=jnp.float32)
        * score_scale
    )
    if allowed is not None:
        scores = jnp.where(allowed[None], scores, floor_score)
    new_max = jnp.maximum(running_max, jnp.max(scores, axis=-1))
    weights = jnp.exp(scores - new_max[:, :, None])
    if allowed is not None:
        weights = jnp.where(allowed[None], weights, 0.0)
    shrink = jnp.exp(running_max - new_max)
    new_sum = running_sum * shrink + jnp.sum(weights, axis=-1)
    added = jnp.einsum(
        "hqk,khe->qhe", weights.astype(jnp.bfloat16), value_rows, preferred_element_type=jnp.float32
    )
    new_acc = running_acc * jnp.transpose(shrink)[:, :, None] + added
    return (new_max, new_sum, new_acc)


def finish(state_now):
    return state_now[2] / jnp.transpose(state_now[1])[:, :, None]


def shards(hits, qkv_weight, out_weight, energy_order, stripe_owner):
    rows_dev, width_dev = hits.shape
    model_width = qkv_weight.shape[0]
    count_ctx = lax.axis_size("ctx")
    my_index = lax.axis_index("ctx")
    heads_dev = width_dev // HEAD_DIM
    score_scale = 1.0 / math.sqrt(HEAD_DIM)
    stripe_len = rows_dev // 2
    per_pair = rows_dev // count_ctx
    pair_owner = jnp.minimum(stripe_owner[:, 0], stripe_owner[:, 1])
    send_rows, take_rows, my_positions = routing(
        energy_order, pair_owner, my_index, rows_dev, count_ctx
    )
    flat_weight = qkv_weight.reshape(model_width, 3 * width_dev)
    outgoing = hits[send_rows].reshape(count_ctx, per_pair, width_dev)
    incoming = lax.all_to_all(outgoing, "ctx", split_axis=0, concat_axis=0, tiled=True)
    arranged = incoming.reshape(count_ctx * per_pair, width_dev)[take_rows]
    projected = jnp.dot(
        lax.all_gather(arranged, "tp", axis=1, tiled=True),
        flat_weight,
        preferred_element_type=jnp.float32,
    ).astype(jnp.bfloat16)
    queries = projected[:, :width_dev].reshape(rows_dev, heads_dev, HEAD_DIM)
    key_value = projected[:, width_dev:]
    low_queries = queries[:stripe_len]
    high_queries = queries[stripe_len:]

    def split_pair(pair_block):
        count_rows = pair_block.shape[0]
        return (
            pair_block[:, :width_dev].reshape(count_rows, heads_dev, HEAD_DIM),
            pair_block[:, width_dev:].reshape(count_rows, heads_dev, HEAD_DIM),
        )

    my_stripe = pair_owner[my_index]
    own_keys, own_values = split_pair(key_value)
    low_allowed = my_positions[None, :stripe_len] <= my_positions[:stripe_len, None]
    high_allowed = my_positions[None, :] <= my_positions[stripe_len:, None]
    low_state = absorb(
        empty_state(heads_dev, stripe_len),
        low_queries,
        own_keys[:stripe_len],
        own_values[:stripe_len],
        low_allowed,
        score_scale,
    )
    high_state = absorb(
        empty_state(heads_dev, stripe_len),
        high_queries,
        own_keys,
        own_values,
        high_allowed,
        score_scale,
    )

    def advance(turn_index, state_now):
        pair_block, low_now, high_now = state_now
        pair_block = passed_along(pair_block, "ctx", 1)
        sender = (my_index - turn_index) % count_ctx
        their_stripe = pair_owner[sender]
        key_rows, value_rows = split_pair(pair_block)
        high_now = absorb(
            high_now,
            high_queries,
            key_rows[:stripe_len],
            value_rows[:stripe_len],
            None,
            score_scale,
        )

        def lower_first():
            return (
                absorb(
                    low_now,
                    low_queries,
                    key_rows[:stripe_len],
                    value_rows[:stripe_len],
                    None,
                    score_scale,
                ),
                high_now,
            )

        def upper_first():
            return (
                low_now,
                absorb(
                    high_now,
                    high_queries,
                    key_rows[stripe_len:],
                    value_rows[stripe_len:],
                    None,
                    score_scale,
                ),
            )

        low_now, high_now = lax.cond(their_stripe < my_stripe, lower_first, upper_first)
        return (pair_block, low_now, high_now)

    moved_block, low_state, high_state = lax.fori_loop(
        1, count_ctx, advance, (key_value, low_state, high_state)
    )
    attended = jnp.concatenate([finish(low_state), finish(high_state)], axis=0)
    merged = attended.astype(jnp.bfloat16).reshape(rows_dev, width_dev)
    my_pair = stripe_owner[my_index]
    swapped = my_pair[0] > my_pair[1]
    merged = jnp.where(swapped, jnp.roll(merged, stripe_len, axis=0), merged)
    mixed = lax.psum_scatter(
        jnp.dot(merged, out_weight, preferred_element_type=jnp.float32).astype(jnp.bfloat16),
        "tp",
        scatter_dimension=0,
        tiled=True,
    )
    return mixed[None]


def layer_kernel(
    hits_ref,
    qkv_ref,
    wout_ref,
    order_hbm,
    owner_hbm,
    out_ref,
    order_ref,
    owner_ref,
    gath,
    wq,
    wmine,
    wtheirs,
    acc,
    proj,
    pick,
    bias,
    qrows,
    att_send,
    att_recv,
    far_send,
    far_recv,
    near,
    local_sem,
    send_sem,
    gath_sem,
    wout_sem,
    att_sem,
    far_sem,
):
    i = lax.axis_index("ctx")
    t = lax.axis_index("tp")
    y = t // 2
    c = t % 2
    oi, oy = 1 - i, 1 - y
    rows, width = hits_ref.shape
    seq = 2 * rows
    half = rows // 2
    quarter = rows // 4
    heads = width // HEAD_DIM
    score_scale = 1.0 / math.sqrt(HEAD_DIM)
    partner = {"ctx": i, "tp": 2 * y + 1 - c}
    x_peer = {"ctx": oi, "tp": t}
    y_peer = {"ctx": i, "tp": 2 * oy + c}
    t_partner = 2 * y + 1 - c
    t_y = 2 * oy + c
    t_diag_partner = 2 * oy + 1 - c

    barrier = pltpu.get_barrier_semaphore()
    for peer in (partner, x_peer, y_peer):
        pl.semaphore_signal(
            barrier, inc=1, device_id=peer, device_id_type=pl.DeviceIdType.MESH
        )

    local = []

    def local_copy(src, dst):
        copy = pltpu.make_async_copy(src, dst, local_sem.at[len(local)])
        copy.start()
        local.append(copy)
        return copy

    hits_in = local_copy(hits_ref, gath.at[i, t])
    order_in = local_copy(order_hbm, order_ref)
    owner_in = local_copy(owner_hbm, owner_ref)
    weight_in = [
        [
            local_copy(
                qkv_ref.at[j, pl.ds(part * 2 * width, 2 * width)],
                wq.at[j, pl.ds(part * 2 * width, 2 * width)],
            )
            for j in range(3)
        ]
        for part in (y, oy)
    ]
    wout_in = local_copy(wout_ref, wmine)

    pl.semaphore_wait(barrier, 3)

    sent = []

    def remote(src, dst, recv, peer):
        copy = pltpu.make_async_remote_copy(
            src_ref=src,
            dst_ref=dst,
            send_sem=send_sem.at[len(sent)],
            recv_sem=recv,
            device_id=peer,
            device_id_type=pl.DeviceIdType.MESH,
        )
        copy.start()
        sent.append(copy)

    def arrived(dst, recv):
        pltpu.make_async_remote_copy(
            src_ref=dst,
            dst_ref=dst,
            send_sem=send_sem.at[0],
            recv_sem=recv,
            device_id=partner,
            device_id_type=pl.DeviceIdType.MESH,
        ).wait_recv()

    def slot(ci, ti, h):
        return gath.at[ci, ti, pl.ds(h * half, half)]

    def own_to(h, peer):
        remote(hits_ref.at[pl.ds(h * half, half)], slot(i, t, h), gath_sem.at[i, t, h], peer)

    def forward(ci, ti, h, peer):
        remote(slot(ci, ti, h), slot(ci, ti, h), gath_sem.at[ci, ti, h], peer)

    def got(ci, ti, h):
        arrived(slot(ci, ti, h), gath_sem.at[ci, ti, h])

    own_to(0, x_peer)
    own_to(1, y_peer)
    own_to(0, partner)
    own_to(1, partner)
    own_to(1, x_peer)
    own_to(0, y_peer)
    remote(wout_ref, wtheirs, wout_sem.at[0], partner)

    order_in.wait()
    owner_in.wait()
    order = order_ref[...].astype(jnp.float32)
    order_rows = jnp.transpose(jnp.broadcast_to(order, (128, seq)))
    entry = lax.broadcasted_iota(jnp.int32, (seq, 128), 0).astype(jnp.float32)
    lane = lax.broadcasted_iota(jnp.int32, (seq, 128), 1)
    row = lax.broadcasted_iota(jnp.int32, (rows, 128), 0)
    first, second = owner_ref[i, 0], owner_ref[i, 1]
    mine_pos = jnp.where(row < half, first * half + row, second * half + row - half).astype(
        jnp.float32
    )
    for block in range(seq // 128):
        cols = pl.ds(block * 128, 128)
        detector = (lane + block * 128).astype(jnp.float32)
        pos = jnp.sum(jnp.where(order_rows == detector, entry, 0.0), axis=0, keepdims=True)
        bias[:, cols] = jnp.where(pos <= mine_pos, 0.0, floor_score)
        pick[:, cols] = jnp.where(pos == mine_pos, score_scale, 0.0).astype(jnp.bfloat16)

    def partial(ci, part, j):
        left = jnp.concatenate([gath[ci, 2 * part], gath[ci, 2 * part + 1]], axis=1)
        right = wq[j, pl.ds(pl.multiple_of(part * 2 * width, 2 * width), 2 * width), :]
        return jnp.dot(left, right, preferred_element_type=jnp.float32)

    def open_rows(ci, which):
        for j in range(3):
            acc[which, j] = partial(ci, y, j)

    def close_rows(ci, which):
        for j in range(3):
            proj[j, pl.ds(pl.multiple_of(ci * rows, rows), rows), :] = (
                acc[which, j] + partial(ci, oy, j)
            ).astype(jnp.bfloat16)

    hits_in.wait()
    for copy in weight_in[0]:
        copy.wait()
    got(i, t_partner, 0)
    got(i, t_partner, 1)
    open_rows(i, 0)

    got(oi, t, 0)
    forward(oi, t, 0, y_peer)
    forward(oi, t, 0, partner)
    got(i, t_y, 1)
    forward(i, t_y, 1, x_peer)
    forward(i, t_y, 1, partner)
    got(oi, t, 1)
    forward(oi, t, 1, partner)
    got(i, t_y, 0)
    forward(i, t_y, 0, partner)

    got(oi, t_partner, 0)
    got(oi, t_partner, 1)
    open_rows(oi, 1)

    got(oi, t_y, 0)
    forward(oi, t_y, 0, partner)
    got(oi, t_y, 1)
    forward(oi, t_y, 1, partner)

    for copy in weight_in[1]:
        copy.wait()
    got(i, t_diag_partner, 0)
    got(i, t_diag_partner, 1)
    close_rows(i, 0)
    got(oi, t_diag_partner, 0)
    got(oi, t_diag_partner, 1)
    close_rows(oi, 1)

    qrows[...] = jnp.dot(pick[...], proj[0], preferred_element_type=jnp.float32)
    head_of = lax.broadcasted_iota(jnp.int32, (quarter, width), 1) // HEAD_DIM

    def attend(owner):
        start = pl.multiple_of(owner * quarter, quarter)
        queries = qrows[pl.ds(start, quarter), :]
        spread = jnp.concatenate(
            [jnp.where(head_of == h, queries, 0.0) for h in range(heads)], axis=0
        ).astype(jnp.bfloat16)
        scores = lax.dot_general(
            spread, proj[1], (((1,), (1,)), ((), ())), preferred_element_type=jnp.float32
        )
        allowed = bias[pl.ds(start, quarter), :]
        scores = scores + jnp.concatenate([allowed] * heads, axis=0)
        weights = jnp.exp(scores - jnp.max(scores, axis=1, keepdims=True))
        total = jnp.sum(weights, axis=1, keepdims=True)
        summed = jnp.dot(
            weights.astype(jnp.bfloat16), proj[2], preferred_element_type=jnp.float32
        ) / total
        merged = jnp.zeros((quarter, width), jnp.float32)
        for h in range(heads):
            merged = jnp.where(head_of == h, summed[h * quarter : (h + 1) * quarter], merged)
        return merged.astype(jnp.bfloat16)

    att_send[0] = attend(t_diag_partner)
    remote(att_send.at[0], att_recv.at[0], att_sem.at[0], partner)
    far_mine = attend(t_y)
    wout_in.wait()
    far_part = jnp.dot(far_mine, wmine[...], preferred_element_type=jnp.float32)
    arrived(wtheirs, wout_sem.at[0])
    arrived(att_recv.at[0], att_sem.at[0])
    far_send[...] = (
        far_part + jnp.dot(att_recv[0], wtheirs[...], preferred_element_type=jnp.float32)
    ).astype(jnp.bfloat16)
    remote(far_send, far_recv, far_sem.at[0], y_peer)

    att_send[1] = attend(t_partner)
    remote(att_send.at[1], att_recv.at[1], att_sem.at[1], partner)
    near[...] = jnp.dot(attend(t), wmine[...], preferred_element_type=jnp.float32)
    arrived(att_recv.at[1], att_sem.at[1])
    near[...] += jnp.dot(att_recv[1], wtheirs[...], preferred_element_type=jnp.float32)
    arrived(far_recv, far_sem.at[0])
    out_ref[...] = (near[...] + far_recv[...].astype(jnp.float32)).astype(jnp.bfloat16)
    for copy in sent:
        copy.wait_send()


def small_slice(hits, qkv_weight, out_weight, energy_order, stripe_owner):
    rows, width = hits.shape
    model_width = qkv_weight.shape[0]
    bf16, f32 = jnp.bfloat16, jnp.float32
    dma = pltpu.SemaphoreType.DMA
    in_hbm = pl.BlockSpec(memory_space=pl.ANY)
    mixed = pl.pallas_call(
        layer_kernel,
        out_shape=pltpu.VMEM((rows // 4, model_width), bf16),
        in_specs=[
            in_hbm,
            in_hbm,
            in_hbm,
            in_hbm,
            in_hbm,
        ],
        out_specs=pl.BlockSpec(memory_space=pltpu.VMEM),
        scratch_shapes=[
            pltpu.VMEM((1, 2 * rows), jnp.int32),
            pltpu.SMEM((2, 2), jnp.int32),
            pltpu.VMEM((2, 4, rows, width), bf16),
            pltpu.VMEM((3, model_width, width), bf16),
            pltpu.VMEM((width, model_width), bf16),
            pltpu.VMEM((width, model_width), bf16),
            pltpu.VMEM((2, 3, rows, width), f32),
            pltpu.VMEM((3, 2 * rows, width), bf16),
            pltpu.VMEM((rows, 2 * rows), bf16),
            pltpu.VMEM((rows, 2 * rows), f32),
            pltpu.VMEM((rows, width), f32),
            pltpu.VMEM((2, rows // 4, width), bf16),
            pltpu.VMEM((2, rows // 4, width), bf16),
            pltpu.VMEM((rows // 4, model_width), bf16),
            pltpu.VMEM((rows // 4, model_width), bf16),
            pltpu.VMEM((rows // 4, model_width), f32),
            dma((10,)),
            dma((18,)),
            dma((2, 4, 2)),
            dma((1,)),
            dma((2,)),
            dma((1,)),
        ],
        compiler_params=pltpu.CompilerParams(
            collective_id=0, has_side_effects=True, vmem_limit_bytes=64000000
        ),
    )(
        hits,
        jnp.transpose(qkv_weight, (1, 0, 2)),
        out_weight,
        energy_order.reshape(1, -1),
        stripe_owner,
    )
    return mixed[None]


def solution(mesh):
    small = mesh.shape["ctx"] == 2 and mesh.shape["tp"] == 4
    placed = (
        P(("batch", "ctx"), "tp"),
        P(None, None, "tp"),
        P("tp", None),
        P("batch"),
        P("batch", None),
    )
    return jax.shard_map(
        small_slice if small else shards,
        mesh=mesh,
        in_specs=placed,
        out_specs=P(("batch", "ctx"), "tp", None),
        check_vma=False,
    )
```

```python
import math

import jax
import jax.numpy as jnp
from jax import lax
from jax.experimental import pallas as pl
from jax.experimental.pallas import tpu as pltpu
from jax.sharding import PartitionSpec as P

HEAD_DIM = 64


floor_score = -1e30


def passed_along(shard, axis, by):
    peers = lax.axis_size(axis)
    return lax.ppermute(shard, axis, [(i, (i + by) % peers) for i in range(peers)])


def stripe_rows(owners, rows_dev, stripes):
    stripe_len = rows_dev // 2
    offsets = jnp.arange(stripe_len, dtype=jnp.int32)
    low_rows = owners[:, None] * stripe_len + offsets[None, :]
    high_rows = (stripes - 1 - owners)[:, None] * stripe_len + offsets[None, :]
    return jnp.concatenate([low_rows, high_rows], axis=1)


def routing(energy_order, pair_owner, my_index, rows_dev, count_ctx):
    every_row = stripe_rows(pair_owner, rows_dev, 2 * count_ctx)
    detector = energy_order[every_row]
    source = detector // rows_dev
    chosen = (source == my_index).astype(jnp.int32)
    ranked = jnp.cumsum(chosen, axis=1) - 1
    per_pair = rows_dev // count_ctx
    slot_ids = jnp.arange(per_pair, dtype=jnp.int32)
    matched = (chosen[:, None, :] == 1) & (ranked[:, None, :] == slot_ids[None, :, None])
    send_rows = jnp.sum(jnp.where(matched, (detector % rows_dev)[:, None, :], 0), axis=-1)
    my_positions = lax.dynamic_index_in_dim(every_row, my_index, 0, keepdims=False)
    mine_source = energy_order[my_positions] // rows_dev
    onehot = (mine_source[:, None] == jnp.arange(count_ctx, dtype=jnp.int32)[None, :]).astype(
        jnp.int32
    )
    mine_rank = jnp.sum((jnp.cumsum(onehot, axis=0) - 1) * onehot, axis=1)
    return (send_rows.reshape(-1), mine_source * per_pair + mine_rank, my_positions)


def empty_state(heads_dev, count_rows):
    return (
        jnp.full((heads_dev, count_rows), floor_score, jnp.float32),
        jnp.zeros((heads_dev, count_rows), jnp.float32),
        jnp.zeros((count_rows, heads_dev, HEAD_DIM), jnp.float32),
    )


def absorb(state_now, queries, key_rows, value_rows, allowed, score_scale):
    running_max, running_sum, running_acc = state_now
    scores = (
        jnp.einsum("qhe,khe->hqk", queries, key_rows, preferred_element_type=jnp.float32)
        * score_scale
    )
    if allowed is not None:
        scores = jnp.where(allowed[None], scores, floor_score)
    new_max = jnp.maximum(running_max, jnp.max(scores, axis=-1))
    weights = jnp.exp(scores - new_max[:, :, None])
    if allowed is not None:
        weights = jnp.where(allowed[None], weights, 0.0)
    shrink = jnp.exp(running_max - new_max)
    new_sum = running_sum * shrink + jnp.sum(weights, axis=-1)
    added = jnp.einsum(
        "hqk,khe->qhe", weights.astype(jnp.bfloat16), value_rows, preferred_element_type=jnp.float32
    )
    new_acc = running_acc * jnp.transpose(shrink)[:, :, None] + added
    return (new_max, new_sum, new_acc)


def finish(state_now):
    return state_now[2] / jnp.transpose(state_now[1])[:, :, None]


def shards(hits, qkv_weight, out_weight, energy_order, stripe_owner):
    rows_dev, width_dev = hits.shape
    model_width = qkv_weight.shape[0]
    count_ctx = lax.axis_size("ctx")
    my_index = lax.axis_index("ctx")
    heads_dev = width_dev // HEAD_DIM
    score_scale = 1.0 / math.sqrt(HEAD_DIM)
    stripe_len = rows_dev // 2
    per_pair = rows_dev // count_ctx
    pair_owner = jnp.minimum(stripe_owner[:, 0], stripe_owner[:, 1])
    send_rows, take_rows, my_positions = routing(
        energy_order, pair_owner, my_index, rows_dev, count_ctx
    )
    flat_weight = qkv_weight.reshape(model_width, 3 * width_dev)
    outgoing = hits[send_rows].reshape(count_ctx, per_pair, width_dev)
    incoming = lax.all_to_all(outgoing, "ctx", split_axis=0, concat_axis=0, tiled=True)
    arranged = incoming.reshape(count_ctx * per_pair, width_dev)[take_rows]
    projected = jnp.dot(
        lax.all_gather(arranged, "tp", axis=1, tiled=True),
        flat_weight,
        preferred_element_type=jnp.float32,
    ).astype(jnp.bfloat16)
    queries = projected[:, :width_dev].reshape(rows_dev, heads_dev, HEAD_DIM)
    key_value = projected[:, width_dev:]
    low_queries = queries[:stripe_len]
    high_queries = queries[stripe_len:]

    def split_pair(pair_block):
        count_rows = pair_block.shape[0]
        return (
            pair_block[:, :width_dev].reshape(count_rows, heads_dev, HEAD_DIM),
            pair_block[:, width_dev:].reshape(count_rows, heads_dev, HEAD_DIM),
        )

    my_stripe = pair_owner[my_index]
    own_keys, own_values = split_pair(key_value)
    low_allowed = my_positions[None, :stripe_len] <= my_positions[:stripe_len, None]
    high_allowed = my_positions[None, :] <= my_positions[stripe_len:, None]
    low_state = absorb(
        empty_state(heads_dev, stripe_len),
        low_queries,
        own_keys[:stripe_len],
        own_values[:stripe_len],
        low_allowed,
        score_scale,
    )
    high_state = absorb(
        empty_state(heads_dev, stripe_len),
        high_queries,
        own_keys,
        own_values,
        high_allowed,
        score_scale,
    )

    def advance(turn_index, state_now):
        pair_block, low_now, high_now = state_now
        pair_block = passed_along(pair_block, "ctx", 1)
        sender = (my_index - turn_index) % count_ctx
        their_stripe = pair_owner[sender]
        key_rows, value_rows = split_pair(pair_block)
        high_now = absorb(
            high_now,
            high_queries,
            key_rows[:stripe_len],
            value_rows[:stripe_len],
            None,
            score_scale,
        )

        def lower_first():
            return (
                absorb(
                    low_now,
                    low_queries,
                    key_rows[:stripe_len],
                    value_rows[:stripe_len],
                    None,
                    score_scale,
                ),
                high_now,
            )

        def upper_first():
            return (
                low_now,
                absorb(
                    high_now,
                    high_queries,
                    key_rows[stripe_len:],
                    value_rows[stripe_len:],
                    None,
                    score_scale,
                ),
            )

        low_now, high_now = lax.cond(their_stripe < my_stripe, lower_first, upper_first)
        return (pair_block, low_now, high_now)

    moved_block, low_state, high_state = lax.fori_loop(
        1, count_ctx, advance, (key_value, low_state, high_state)
    )
    attended = jnp.concatenate([finish(low_state), finish(high_state)], axis=0)
    merged = attended.astype(jnp.bfloat16).reshape(rows_dev, width_dev)
    my_pair = stripe_owner[my_index]
    swapped = my_pair[0] > my_pair[1]
    merged = jnp.where(swapped, jnp.roll(merged, stripe_len, axis=0), merged)
    mixed = lax.psum_scatter(
        jnp.dot(merged, out_weight, preferred_element_type=jnp.float32).astype(jnp.bfloat16),
        "tp",
        scatter_dimension=0,
        tiled=True,
    )
    return mixed[None]


def layer_kernel(
    hits_ref,
    qkv_ref,
    wout_ref,
    order_hbm,
    owner_hbm,
    out_ref,
    order_ref,
    owner_ref,
    gath,
    wq,
    wmine,
    wtheirs,
    acc,
    proj,
    pick,
    bias,
    qrows,
    att_send,
    att_recv,
    far_send,
    far_recv,
    near,
    local_sem,
    send_sem,
    gath_sem,
    wout_sem,
    att_sem,
    far_sem,
):
    i = lax.axis_index("ctx")
    t = lax.axis_index("tp")
    y = t // 2
    c = t % 2
    oi, oy = 1 - i, 1 - y
    rows, width = hits_ref.shape
    seq = 2 * rows
    half = rows // 2
    quarter = rows // 4
    heads = width // HEAD_DIM
    score_scale = 1.0 / math.sqrt(HEAD_DIM)
    partner = {"ctx": i, "tp": 2 * y + 1 - c}
    x_peer = {"ctx": oi, "tp": t}
    y_peer = {"ctx": i, "tp": 2 * oy + c}
    t_partner = 2 * y + 1 - c
    t_y = 2 * oy + c
    t_diag_partner = 2 * oy + 1 - c

    barrier = pltpu.get_barrier_semaphore()
    for peer in (partner, x_peer, y_peer):
        pl.semaphore_signal(
            barrier, inc=1, device_id=peer, device_id_type=pl.DeviceIdType.MESH
        )

    local = []

    def local_copy(src, dst):
        copy = pltpu.make_async_copy(src, dst, local_sem.at[len(local)])
        copy.start()
        local.append(copy)
        return copy

    hits_in = local_copy(hits_ref, gath.at[i, t])
    order_in = local_copy(order_hbm, order_ref)
    owner_in = local_copy(owner_hbm, owner_ref)
    weight_in = [
        local_copy(
            qkv_ref.at[:, pl.ds(part * 2 * width, 2 * width)],
            wq.at[:, pl.ds(part * 2 * width, 2 * width)],
        )
        for part in (y, oy)
    ]
    wout_in = local_copy(wout_ref, wmine)

    pl.semaphore_wait(barrier, 3)

    sent = []

    def remote(src, dst, recv, peer):
        copy = pltpu.make_async_remote_copy(
            src_ref=src,
            dst_ref=dst,
            send_sem=send_sem.at[len(sent)],
            recv_sem=recv,
            device_id=peer,
            device_id_type=pl.DeviceIdType.MESH,
        )
        copy.start()
        sent.append(copy)

    def arrived(dst, recv):
        pltpu.make_async_remote_copy(
            src_ref=dst,
            dst_ref=dst,
            send_sem=send_sem.at[0],
            recv_sem=recv,
            device_id=partner,
            device_id_type=pl.DeviceIdType.MESH,
        ).wait_recv()

    first, second, third, fourth = ((k * quarter, quarter) for k in range(4))
    low, high, whole = (0, half), (half, half), (0, rows)
    chunk_sem = {first: 0, second: 1, third: 2, fourth: 3, low: 0, high: 2, whole: 0}

    def slot(ci, ti, chunk):
        return gath.at[ci, ti, pl.ds(*chunk)], gath_sem.at[ci, ti, chunk_sem[chunk]]

    def own_to(peer, chunk):
        remote(hits_ref.at[pl.ds(*chunk)], *slot(i, t, chunk), peer)

    def forward(ci, ti, chunk, *peers):
        arrived(*slot(ci, ti, chunk))
        for peer in peers:
            remote(slot(ci, ti, chunk)[0], *slot(ci, ti, chunk), peer)

    def got(ci, ti, *chunks):
        for chunk in chunks:
            arrived(*slot(ci, ti, chunk))

    own_to(x_peer, first)
    own_to(y_peer, fourth)
    own_to(x_peer, second)
    own_to(y_peer, third)
    own_to(partner, whole)
    own_to(x_peer, high)
    own_to(y_peer, low)
    remote(wout_ref, wtheirs, wout_sem.at[0], partner)

    order_in.wait()
    owner_in.wait()
    order = order_ref[...].astype(jnp.float32)
    order_rows = jnp.transpose(jnp.broadcast_to(order, (128, seq)))
    entry = lax.broadcasted_iota(jnp.int32, (seq, 128), 0).astype(jnp.float32)
    lane = lax.broadcasted_iota(jnp.int32, (seq, 128), 1)
    row = lax.broadcasted_iota(jnp.int32, (rows, 128), 0)
    stripe_a, stripe_b = owner_ref[i, 0], owner_ref[i, 1]
    mine_pos = jnp.where(row < half, stripe_a * half + row, stripe_b * half + row - half).astype(
        jnp.float32
    )
    for block in range(seq // 128):
        cols = pl.ds(block * 128, 128)
        detector = (lane + block * 128).astype(jnp.float32)
        pos = jnp.sum(jnp.where(order_rows == detector, entry, 0.0), axis=0, keepdims=True)
        bias[:, cols] = jnp.where(pos <= mine_pos, 0.0, floor_score)
        pick[:, cols] = jnp.where(pos == mine_pos, score_scale, 0.0).astype(jnp.bfloat16)

    def partial(ci, part, j):
        left = jnp.concatenate([gath[ci, 2 * part], gath[ci, 2 * part + 1]], axis=1)
        right = wq[j, pl.ds(pl.multiple_of(part * 2 * width, 2 * width), 2 * width), :]
        return jnp.dot(left, right, preferred_element_type=jnp.float32)

    def open_rows(ci, which):
        for j in range(3):
            acc[which, j] = partial(ci, y, j)

    def close_rows(ci, which):
        for j in range(3):
            proj[j, pl.ds(pl.multiple_of(ci * rows, rows), rows), :] = (
                acc[which, j] + partial(ci, oy, j)
            ).astype(jnp.bfloat16)

    hits_in.wait()
    weight_in[0].wait()
    got(i, t_partner, whole)
    open_rows(i, 0)

    forward(oi, t, first, y_peer)
    forward(i, t_y, fourth, x_peer)
    forward(oi, t, second, y_peer)
    forward(i, t_y, third, x_peer)
    remote(slot(oi, t, low)[0], *slot(oi, t, low), partner)
    remote(slot(i, t_y, high)[0], *slot(i, t_y, high), partner)
    forward(oi, t, high, partner)
    forward(i, t_y, low, partner)

    got(oi, t_partner, low, high)
    open_rows(oi, 1)

    forward(oi, t_y, first, partner)
    forward(oi, t_y, fourth, partner)
    forward(oi, t_y, second, partner)
    forward(oi, t_y, third, partner)

    weight_in[1].wait()
    got(i, t_diag_partner, low, high)
    close_rows(i, 0)
    got(oi, t_diag_partner, first, fourth, second, third)
    close_rows(oi, 1)

    qrows[...] = jnp.dot(pick[...], proj[0], preferred_element_type=jnp.float32)
    head_of = lax.broadcasted_iota(jnp.int32, (quarter, width), 1) // HEAD_DIM

    def attend(owner):
        start = pl.multiple_of(owner * quarter, quarter)
        queries = qrows[pl.ds(start, quarter), :]
        spread = jnp.concatenate(
            [jnp.where(head_of == h, queries, 0.0) for h in range(heads)], axis=0
        ).astype(jnp.bfloat16)
        scores = lax.dot_general(
            spread, proj[1], (((1,), (1,)), ((), ())), preferred_element_type=jnp.float32
        )
        allowed = bias[pl.ds(start, quarter), :]
        scores = scores + jnp.concatenate([allowed] * heads, axis=0)
        weights = jnp.exp(scores - jnp.max(scores, axis=1, keepdims=True))
        total = jnp.sum(weights, axis=1, keepdims=True)
        summed = jnp.dot(
            weights.astype(jnp.bfloat16), proj[2], preferred_element_type=jnp.float32
        ) / total
        merged = jnp.zeros((quarter, width), jnp.float32)
        for h in range(heads):
            merged = jnp.where(head_of == h, summed[h * quarter : (h + 1) * quarter], merged)
        return merged.astype(jnp.bfloat16)

    att_send[0] = attend(t_diag_partner)
    remote(att_send.at[0], att_recv.at[0], att_sem.at[0], partner)
    far_mine = attend(t_y)
    wout_in.wait()
    far_part = jnp.dot(far_mine, wmine[...], preferred_element_type=jnp.float32)
    arrived(wtheirs, wout_sem.at[0])
    arrived(att_recv.at[0], att_sem.at[0])
    cut = far_send.shape[1] // 2
    for side in range(2):
        cols = slice(side * cut, (side + 1) * cut)
        far_send[:, cols] = (
            far_part[:, cols]
            + jnp.dot(att_recv[0], wtheirs[:, cols], preferred_element_type=jnp.float32)
        ).astype(jnp.bfloat16)
        remote(far_send.at[:, cols], far_recv.at[:, cols], far_sem.at[side], y_peer)

    att_send[1] = attend(t_partner)
    remote(att_send.at[1], att_recv.at[1], att_sem.at[1], partner)
    near[...] = jnp.dot(attend(t), wmine[...], preferred_element_type=jnp.float32)
    arrived(att_recv.at[1], att_sem.at[1])
    near[...] += jnp.dot(att_recv[1], wtheirs[...], preferred_element_type=jnp.float32)
    for copy in sent:
        copy.wait_send()
    for side in range(2):
        cols = slice(side * cut, (side + 1) * cut)
        arrived(far_recv.at[:, cols], far_sem.at[side])
        out_ref[:, cols] = (near[:, cols] + far_recv[:, cols].astype(jnp.float32)).astype(
            jnp.bfloat16
        )


def small_slice(hits, qkv_weight, out_weight, energy_order, stripe_owner):
    rows, width = hits.shape
    model_width = qkv_weight.shape[0]
    bf16, f32 = jnp.bfloat16, jnp.float32
    dma = pltpu.SemaphoreType.DMA
    in_hbm = pl.BlockSpec(memory_space=pl.ANY)
    mixed = pl.pallas_call(
        layer_kernel,
        out_shape=pltpu.VMEM((rows // 4, model_width), bf16),
        in_specs=[
            in_hbm,
            in_hbm,
            in_hbm,
            in_hbm,
            in_hbm,
        ],
        out_specs=pl.BlockSpec(memory_space=pltpu.VMEM),
        scratch_shapes=[
            pltpu.VMEM((1, 2 * rows), jnp.int32),
            pltpu.SMEM((2, 2), jnp.int32),
            pltpu.VMEM((2, 4, rows, width), bf16),
            pltpu.VMEM((3, model_width, width), bf16),
            pltpu.VMEM((width, model_width), bf16),
            pltpu.VMEM((width, model_width), bf16),
            pltpu.VMEM((2, 3, rows, width), f32),
            pltpu.VMEM((3, 2 * rows, width), bf16),
            pltpu.VMEM((rows, 2 * rows), bf16),
            pltpu.VMEM((rows, 2 * rows), f32),
            pltpu.VMEM((rows, width), f32),
            pltpu.VMEM((2, rows // 4, width), bf16),
            pltpu.VMEM((2, rows // 4, width), bf16),
            pltpu.VMEM((rows // 4, model_width), bf16),
            pltpu.VMEM((rows // 4, model_width), bf16),
            pltpu.VMEM((rows // 4, model_width), f32),
            dma((6,)),
            dma((24,)),
            dma((2, 4, 4)),
            dma((1,)),
            dma((2,)),
            dma((2,)),
        ],
        compiler_params=pltpu.CompilerParams(
            collective_id=0, has_side_effects=True, vmem_limit_bytes=64000000
        ),
    )(
        hits,
        jnp.transpose(qkv_weight, (1, 0, 2)),
        out_weight,
        energy_order.reshape(1, -1),
        stripe_owner,
    )
    return mixed[None]


def solution(mesh):
    small = mesh.shape["ctx"] == 2 and mesh.shape["tp"] == 4
    placed = (
        P(("batch", "ctx"), "tp"),
        P(None, None, "tp"),
        P("tp", None),
        P("batch"),
        P("batch", None),
    )
    return jax.shard_map(
        small_slice if small else shards,
        mesh=mesh,
        in_specs=placed,
        out_specs=P(("batch", "ctx"), "tp", None),
        check_vma=False,
    )
```
